256 devices in a mesh: section: 8 (over x, core), dp: 32 (over y, z).
Axes of the slice: x: 4, y: 4, z: 8, core: 2. Of those that a mesh axis runs over, the one named last changes fastest.
Arguments:
- inputs: bfloat16 [2, 4096, 1536], P(None, 'dp'), may hold values from -6 to 6
- grad_out: bfloat16 [2, 4096, 1536], P(None, 'dp'), may hold values from -6 to 6
- w_conv: bfloat16 [8, 4608, 768], P('section'), may hold values from -0.09375 to 0.09375
- w_point: bfloat16 [8, 768, 1536], P('section'), may hold values from -0.21875 to 0.21875
- gain_conv: float32 [8, 1536], P('section'), may hold values from 0.25 to 1.75
- gain_point: float32 [8, 768], P('section'), may hold values from 0.25 to 1.75
Outputs:
- grad_w_conv: float32 [8, 4608, 768], P('section', 'dp')
- grad_w_point: float32 [8, 768, 1536], P('section', 'dp')
- grad_gain_conv: float32 [8, 1536], P('section', 'dp')
- grad_gain_point: float32 [8, 768], P('section', 'dp')
- grad_acts: bfloat16 [8, 2, 4096, 1536], P('section', None, 'dp')
The draws below stay inside these ranges and needn't reach their ends.
All inputs are finite; a program needn't handle non-finite values.
Results may differ from the reference program's by a relative error of at most 0.034.
Values may be sent and summed in bfloat16 or wider, within the bound.
No kernel may reach another device: no remote copies, remote signals or barrier semaphores. Data moves between devices by JAX's collectives and lax.ppermute only.
A program may use at most 128 MiB of HBM per device.

```python
import math
import jax
import jax.numpy as jnp
from jax import lax

C = 1536
M = 768
MB = 2
SECTIONS = 8
LEN = 4096
N_SECTION = 8


def block_levels(stream_key, dims, shards, least, high):
    level, own = 1.0, jax.random.fold_in(stream_key, 6)
    for dim, shards_of in shards:
        steps = jnp.exp(jax.random.uniform(jax.random.fold_in(own, dim), (shards_of,), jnp.float32, least / len(shards), high / len(shards)))
        level = level * jnp.repeat(steps, dims[dim] // shards_of).reshape([-1 if axis == dim else 1 for axis in range(len(dims))])
    return level


def noise(stream_key, extent, scale, most, cuts=(), held_as=jnp.bfloat16):
    entries = scale * jax.random.normal(stream_key, extent, jnp.float32)
    if cuts:
        entries = entries * block_levels(stream_key, extent, cuts, -0.22, 0.18)
    return jnp.clip(entries, -most, most).astype(held_as)


def setup_inputs(seed: int = 0) -> dict:
    key_list = jax.random.split(jax.random.key(seed), 7)
    inputs = noise(key_list[0], (MB, LEN, C), 1.0, 6.0, ((1, 32),))
    grad_out = noise(key_list[1], (MB, LEN, C), 1.0, 6.0, ((1, 32),))
    w_conv = noise(key_list[2], (SECTIONS, 3 * C, M), (3 * C) ** -0.5, 0.09375, ((0, 8),))
    w_point = noise(key_list[3], (SECTIONS, M, C), M ** -0.5, 0.21875, ((0, 8),))
    gain_conv = jnp.clip(1.0 + 0.15 * jax.random.normal(key_list[4], (SECTIONS, C), jnp.float32), 0.25, 1.75)
    gain_point = jnp.clip(1.0 + 0.15 * jax.random.normal(key_list[5], (SECTIONS, M), jnp.float32), 0.25, 1.75)
    return dict(inputs=inputs, grad_out=grad_out, w_conv=w_conv, w_point=w_point, gain_conv=gain_conv, gain_point=gain_point)


EPSILON = 1e-06

def norm_act(values, scales):
    mean_sq = lax.optimization_barrier(jnp.mean(values * values, axis=-1, keepdims=True))
    return jax.nn.gelu(values * lax.rsqrt(mean_sq + EPSILON) * scales)

def shifted(values, dilation, offset):
    margin_rows = values.shape[1] // 2
    padded = jnp.pad(values, ((0, 0), (margin_rows, margin_rows), (0, 0)))
    return lax.dynamic_slice_in_dim(padded, margin_rows + offset * dilation, values.shape[1], 1)

def unfold(activations, dilation):
    joined = jnp.concatenate([shifted(activations, dilation, -1), activations, shifted(activations, dilation, 1)], axis=-1)
    return joined.reshape(-1, joined.shape[-1])

def block_forward(incoming, weight_conv, weight_point, scale_conv, scale_point, dilation):
    batches, positions, channels = incoming.shape
    widened = incoming.astype(jnp.float32)
    activations = norm_act(widened, scale_conv).astype(jnp.bfloat16)
    columns = unfold(activations, dilation)
    conv_out = jnp.dot(columns, weight_conv, preferred_element_type=jnp.float32)
    mixture = norm_act(conv_out, scale_point).astype(jnp.bfloat16)
    branch = jnp.dot(mixture, weight_point, preferred_element_type=jnp.float32)
    outputs = (widened.reshape(-1, channels) + branch).astype(jnp.bfloat16)
    return (outputs.reshape(batches, positions, channels), conv_out)

def block_backward(incoming, conv_out, upstream, weight_conv, weight_point, scale_conv, scale_point, dilation):
    batches, positions, channels = incoming.shape
    widened = incoming.astype(jnp.float32)
    acts_wide, pull_conv = jax.vjp(norm_act, widened, scale_conv)
    activations = acts_wide.astype(jnp.bfloat16)
    columns = unfold(activations, dilation)
    mix_wide, pull_point = jax.vjp(norm_act, conv_out, scale_point)
    mixture = mix_wide.astype(jnp.bfloat16)
    flat_up = upstream.reshape(-1, channels)
    grad_point = jnp.dot(mixture.T, flat_up, preferred_element_type=jnp.float32)
    grad_mixture = jnp.dot(flat_up, weight_point.T, preferred_element_type=jnp.float32)
    grad_conv_wide, grad_scale_point = pull_point(grad_mixture)
    grad_conv = grad_conv_wide.astype(jnp.bfloat16)
    grad_wconv = jnp.dot(columns.T, grad_conv, preferred_element_type=jnp.float32)
    grad_cols = jnp.dot(grad_conv, weight_conv.T, preferred_element_type=jnp.float32)
    grad_cols = grad_cols.reshape(batches, positions, 3 * channels)
    grad_acts = shifted(grad_cols[:, :, :channels], dilation, 1)
    grad_acts = grad_acts + grad_cols[:, :, channels:2 * channels]
    grad_acts = grad_acts + shifted(grad_cols[:, :, 2 * channels:], dilation, -1)
    grad_widened, grad_scale_conv = pull_conv(grad_acts)
    downstream = (upstream.astype(jnp.float32) + grad_widened).astype(jnp.bfloat16)
    return (downstream, grad_wconv, grad_point, grad_scale_conv, grad_scale_point)

def reference(inputs, grad_out, w_conv, w_point, gain_conv, gain_point):
    stored = []
    stored_conv = []
    current = inputs
    for layer_index in range(N_SECTION):
        dilation = 3 ** layer_index // 2 ** layer_index
        stored.append(current)
        current, conv_out = block_forward(current, w_conv[layer_index], w_point[layer_index], gain_conv[layer_index], gain_point[layer_index], dilation)
        stored_conv.append(conv_out)
    upstream = grad_out
    conv_grads = [None] * N_SECTION
    point_grads = [None] * N_SECTION
    gconv_grads = [None] * N_SECTION
    gpoint_grads = [None] * N_SECTION
    input_grads = [None] * N_SECTION
    for layer_index in reversed(range(N_SECTION)):
        dilation = 3 ** layer_index // 2 ** layer_index
        upstream, grad_wconv, grad_point, grad_sc, grad_sp = block_backward(stored[layer_index], stored_conv[layer_index], upstream, w_conv[layer_index], w_point[layer_index], gain_conv[layer_index], gain_point[layer_index], dilation)
        conv_grads[layer_index] = grad_wconv
        point_grads[layer_index] = grad_point
        gconv_grads[layer_index] = grad_sc
        gpoint_grads[layer_index] = grad_sp
        input_grads[layer_index] = upstream
    norm_scale = 1.0 / math.sqrt(inputs.shape[0] * inputs.shape[1])
    return (jnp.stack(conv_grads) * norm_scale, jnp.stack(point_grads) * norm_scale, jnp.stack(gconv_grads) * norm_scale, jnp.stack(gpoint_grads) * norm_scale, jnp.stack(input_grads))
```

```python
import math

import jax
import jax.numpy as jnp
from jax import lax
from jax.sharding import PartitionSpec as P

EPSILON = 1e-06
Y_CHIPS = 4
GELU_SCALE = math.sqrt(2.0 / math.pi)
GELU_CUBIC = 0.044715


def normed(values):
    inverse = lax.rsqrt(jnp.mean(values * values, axis=-1, keepdims=True) + EPSILON)
    return values * inverse, inverse


def gelu_and_slope(u):
    tanh = jnp.tanh(GELU_SCALE * (u + GELU_CUBIC * u * u * u))
    half = 0.5 * (1.0 + tanh)
    slope = half + 0.5 * u * (1.0 - tanh * tanh) * GELU_SCALE * (1.0 + 3.0 * GELU_CUBIC * u * u)
    return u * half, slope


def act(values, gain):
    hat, unused = normed(values)
    return gelu_and_slope(hat * gain)[0]


def matmul(left, right):
    return lax.dot_general(
        left, right, (((left.ndim - 1,), (0,)), ((), ())), preferred_element_type=jnp.float32
    )


def matmul_t(left, right):
    return lax.dot_general(
        left, right, (((left.ndim - 1,), (1,)), ((), ())), preferred_element_type=jnp.float32
    )


def halo(rows, width, dp):
    left = lax.ppermute(rows[:, -width:], "dp", [(i, i + 1) for i in range(dp - 1)])
    right = lax.ppermute(rows[:, :width], "dp", [(i + 1, i) for i in range(dp - 1)])
    return left, right


def on_device(inputs, grad_out, w_conv, w_point, gain_conv, gain_point):
    micro, positions, channels = inputs.shape
    section = lax.axis_index("section")
    sections = lax.axis_size("section")
    dp_index = lax.axis_index("dp")
    dp = lax.axis_size("dp")
    ny = Y_CHIPS
    nz = dp // ny
    y_groups = [[y * nz + z for y in range(ny)] for z in range(nz)]
    z_groups = [[y * nz + z for z in range(nz)] for y in range(ny)]
    length = positions * dp
    norm_scale = 1.0 / math.sqrt(micro * length)
    dil = [3**s // 2**s for s in range(sections)]
    reach = dil[-1]
    ahead = [sum(dil[s : sections - 1]) for s in range(sections)]
    back = [sum(dil[:s]) for s in range(sections + 1)]
    wide = back[sections]
    outer = wide + reach
    dilation = jnp.array(dil, jnp.int32)[section]
    inner = w_conv.shape[2]
    weight_conv = w_conv[0]
    taps = weight_conv.reshape(3, channels, inner)
    weight_point = w_point[0]
    g_conv = gain_conv[0][None]
    g_point = gain_point[0][None]

    def inside(ext):
        place = lax.broadcasted_iota(jnp.int32, (positions + 2 * ext, 1), 0) + (
            dp_index * positions - ext
        )
        return (place >= 0) & (place < length)

    def hop(rows, source, target):
        pairs = [(source * dp + i, target * dp + i) for i in range(dp)]
        return lax.ppermute(rows, ("section", "dp"), pairs)

    left, right = halo(inputs, ahead[0], dp)
    current = [jnp.concatenate([left[m], inputs[m], right[m]], axis=0) for m in range(micro)]
    kept = [inputs[m] for m in range(micro)]
    for s in range(sections - 1):
        rows = positions + 2 * ahead[s + 1]
        d = dil[s]
        for m in range(micro):
            wide_x = current[m].astype(jnp.float32)
            a = act(wide_x, g_conv).astype(jnp.bfloat16)
            conv = matmul(a[:rows], taps[0])
            conv = conv + matmul(a[d : d + rows], taps[1])
            conv = conv + matmul(a[2 * d : 2 * d + rows], taps[2])
            b = act(conv, g_point).astype(jnp.bfloat16)
            out = (wide_x[d : d + rows] + matmul(b, weight_point)).astype(jnp.bfloat16)
            out = jnp.where(inside(ahead[s + 1]), out, jnp.zeros_like(out))
            current[m] = hop(out, s, s + 1)
            mine = current[m][ahead[s + 1] : ahead[s + 1] + positions]
            kept[m] = jnp.where(section == s + 1, mine, kept[m])

    x_main = jnp.stack(kept)
    left, right = halo(x_main, outer, dp)
    x_ext = jnp.concatenate([left, x_main, right], axis=1)
    x_wide = x_ext.astype(jnp.float32)
    x_hat, x_inv = normed(x_wide)
    a_wide, x_slope = gelu_and_slope(x_hat * g_conv)
    a_ext = a_wide.astype(jnp.bfloat16)
    conv_rows = positions + 2 * wide

    def tap_rows(array, start, count, dim):
        return [
            lax.dynamic_slice_in_dim(array, start + (k - 1) * dilation, count, dim)
            for k in range(3)
        ]

    columns = tap_rows(a_ext, outer - wide, conv_rows, 1)
    conv = sum(matmul(columns[k], taps[k]) for k in range(3))
    v_hat, v_inv = normed(conv)
    b_wide, v_slope = gelu_and_slope(v_hat * g_point)
    b_main = b_wide[:, wide : wide + positions].astype(jnp.bfloat16)
    core = slice(outer - back[sections - 1], outer + positions + back[sections - 1])
    x_res = lax.optimization_barrier((x_hat[:, core], x_inv[:, core], x_slope[:, core]))
    v_res = lax.optimization_barrier((v_hat, v_inv, v_slope))
    x_hat, x_inv, x_slope = x_res
    v_hat, v_inv, v_slope = v_res

    a_send = a_ext[:, outer - reach : outer + positions + reach]
    a_all = lax.all_gather(a_send, "dp", axis=0, axis_index_groups=y_groups)
    b_all = lax.all_gather(b_main, "dp", axis=0, axis_index_groups=y_groups)
    count = ny * micro * positions
    a_cols = tap_rows(a_all, reach, positions, 2)
    a_cols = jnp.concatenate([c.reshape(count, channels) for c in a_cols], axis=1)
    b_cols = b_all.reshape(count, inner)

    def act_pull(grad, gain, hat, inverse, slope):
        w = grad * slope * gain
        return inverse * (w - hat * jnp.mean(w * hat, axis=-1, keepdims=True))

    left, right = halo(grad_out, wide, dp)
    current = [jnp.concatenate([left[m], grad_out[m], right[m]], axis=0) for m in range(micro)]
    zero_q = jnp.zeros((positions + 2 * reach, inner), jnp.bfloat16)
    kept_in = [grad_out[m] for m in range(micro)]
    kept_q = [zero_q for m in range(micro)]
    kept_out = [grad_out[m] for m in range(micro)]
    for s in reversed(range(sections)):
        rows = positions + 2 * back[s]
        d = dil[s]
        here = section == s
        for m in range(micro):
            e = current[m]
            part = slice(wide - back[s + 1], wide + positions + back[s + 1])
            grad_b = matmul_t(e, weight_point)
            q = act_pull(grad_b, g_point, v_hat[m, part], v_inv[m, part], v_slope[m, part])
            q = q.astype(jnp.bfloat16)
            r = matmul_t(q[2 * d : 2 * d + rows], taps[0])
            r = r + matmul_t(q[d : d + rows], taps[1])
            r = r + matmul_t(q[:rows], taps[2])
            base = back[sections - 1]
            part = slice(base - back[s], base + positions + back[s])
            t = act_pull(r, g_conv, x_hat[m, part], x_inv[m, part], x_slope[m, part])
            out = (e[d : d + rows].astype(jnp.float32) + t).astype(jnp.bfloat16)
            out = jnp.where(inside(back[s]), out, jnp.zeros_like(out))
            if s > 0:
                current[m] = hop(out, s, s - 1)
            ext = back[s + 1]
            if ext >= reach:
                mine_q = q[ext - reach : ext + positions + reach]
            else:
                mine_q = jnp.pad(q, ((reach - ext, reach - ext), (0, 0)))
            kept_q[m] = jnp.where(here, mine_q, kept_q[m])
            kept_in[m] = jnp.where(here, e[ext : ext + positions], kept_in[m])
            kept_out[m] = jnp.where(here, out[back[s] : back[s] + positions], kept_out[m])

    q_keep = jnp.stack(kept_q)
    e_keep = jnp.stack(kept_in)
    grad_acts = jnp.stack(kept_out)
    q_main = q_keep[:, reach : reach + positions].reshape(micro * positions, inner)
    e_main = e_keep.reshape(micro * positions, channels)

    def column_blocks(array):
        blocks = array.reshape(array.shape[0], ny, array.shape[1] // ny)
        return blocks.transpose(1, 0, 2)

    def swap_y(array):
        return lax.all_to_all(array, "dp", 0, 0, axis_index_groups=y_groups)

    q_part = inner // ny
    send = jnp.concatenate([column_blocks(q_main), column_blocks(e_main)], axis=2)
    got = swap_y(send).reshape(count, q_part + channels // ny)
    q_got, e_got = got[:, :q_part], got[:, q_part:]

    def contract(left, right):
        return lax.dot_general(
            left, right, (((0,), (0,)), ((), ())), preferred_element_type=jnp.float32
        )

    grad_conv = contract(a_cols, q_got).astype(jnp.bfloat16)
    grad_point = contract(b_cols, e_got).astype(jnp.bfloat16)
    conv_own = 3 * channels // dp
    point_own = inner // dp
    half = conv_own // 2
    conv_pack = grad_conv.reshape(ny, nz, 2, half, q_part)
    pack = jnp.concatenate(
        [
            jnp.concatenate([conv_pack[:, :, 0], conv_pack[:, :, 1]], axis=-1),
            grad_point.reshape(ny, nz, point_own, channels // ny),
        ],
        axis=2,
    )
    pack = pack.transpose(1, 0, 2, 3).reshape(nz * ny * (half + point_own), 2 * q_part)
    total = lax.psum_scatter(
        pack, "dp", scatter_dimension=0, axis_index_groups=z_groups, tiled=True
    ).reshape(ny, half + point_own, 2 * q_part)

    q_late, e_late, unused = lax.optimization_barrier((q_keep, e_keep, pack))
    mid = slice(wide, wide + positions)
    grad_b = matmul_t(e_late, weight_point)
    gain_p = jnp.sum(grad_b * v_slope[:, mid] * v_hat[:, mid], axis=(0, 1))
    q_cols = tap_rows(q_late, reach, positions, 1)
    r = sum(matmul_t(q_cols[2 - k], taps[k]) for k in range(3))
    mid = slice(back[sections - 1], back[sections - 1] + positions)
    gain_c = jnp.sum(r * x_slope[:, mid] * x_hat[:, mid], axis=(0, 1))
    gains = jnp.concatenate(
        [gain_c.reshape(dp, channels // dp), gain_p.reshape(dp, inner // dp)], axis=1
    )
    gains = gains.reshape(ny, nz, -1).transpose(1, 0, 2)
    gains = lax.all_to_all(gains, "dp", 0, 0, axis_index_groups=z_groups).sum(0)
    gains = swap_y(gains).sum(0) * norm_scale

    own = swap_y(total).astype(jnp.float32) * norm_scale
    own_conv = own[:, :half].reshape(ny, half, 2, q_part)
    own_conv = own_conv.transpose(2, 1, 0, 3).reshape(conv_own, inner)
    own_point = own[:, half:].transpose(1, 0, 2).reshape(point_own, channels)
    return (
        own_conv[None],
        own_point[None],
        gains[: channels // dp][None],
        gains[channels // dp :][None],
        grad_acts[None],
    )


def solution(mesh):
    return jax.shard_map(
        on_device,
        mesh=mesh,
        in_specs=(
            P(None, "dp", None),
            P(None, "dp", None),
            P("section", None, None),
            P("section", None, None),
            P("section", None),
            P("section", None),
        ),
        out_specs=(
            P("section", "dp", None),
            P("section", "dp", None),
            P("section", "dp"),
            P("section", "dp"),
            P("section", None, "dp", None),
        ),
        check_vma=False,
    )
```

```python
import math

import jax
import jax.numpy as jnp
from jax import lax
from jax.sharding import PartitionSpec as P

EPSILON = 1e-06
Y_CHIPS = 4
GELU_SCALE = math.sqrt(2.0 / math.pi)
GELU_CUBIC = 0.044715


def normed(values):
    inverse = lax.rsqrt(jnp.mean(values * values, axis=-1, keepdims=True) + EPSILON)
    return values * inverse, inverse


def gelu_and_slope(u):
    tanh = jnp.tanh(GELU_SCALE * (u + GELU_CUBIC * u * u * u))
    half = 0.5 * (1.0 + tanh)
    slope = half + 0.5 * u * (1.0 - tanh * tanh) * GELU_SCALE * (1.0 + 3.0 * GELU_CUBIC * u * u)
    return u * half, slope


def act(values, gain):
    hat, unused = normed(values)
    return gelu_and_slope(hat * gain)[0]


def matmul(left, right):
    return lax.dot_general(
        left, right, (((left.ndim - 1,), (0,)), ((), ())), preferred_element_type=jnp.float32
    )


def matmul_t(left, right):
    return lax.dot_general(
        left, right, (((left.ndim - 1,), (1,)), ((), ())), preferred_element_type=jnp.float32
    )


def halo(rows, width, dp):
    left = lax.ppermute(rows[:, -width:], "dp", [(i, i + 1) for i in range(dp - 1)])
    right = lax.ppermute(rows[:, :width], "dp", [(i + 1, i) for i in range(dp - 1)])
    return left, right


def on_device(inputs, grad_out, w_conv, w_point, gain_conv, gain_point):
    micro, positions, channels = inputs.shape
    section = lax.axis_index("section")
    sections = lax.axis_size("section")
    dp_index = lax.axis_index("dp")
    dp = lax.axis_size("dp")
    ny = Y_CHIPS
    nz = dp // ny
    y_groups = [[y * nz + z for y in range(ny)] for z in range(nz)]
    z_groups = [[y * nz + z for z in range(nz)] for y in range(ny)]
    length = positions * dp
    norm_scale = 1.0 / math.sqrt(micro * length)
    dil = [3**s // 2**s for s in range(sections)]
    reach = dil[-1]
    ahead = [sum(dil[s : sections - 1]) for s in range(sections)]
    ahead[0] = -(-ahead[0] // 16) * 16
    back = [sum(dil[:s]) for s in range(sections + 1)]
    wide = back[sections]
    outer = wide + reach
    dilation = sum(jnp.where(section == s, dil[s], 0) for s in range(sections))
    inner = w_conv.shape[2]
    weight_conv = w_conv[0]
    taps = weight_conv.reshape(3, channels, inner)
    weight_point = w_point[0]
    g_conv = gain_conv[0][None]
    g_point = gain_point[0][None]

    def masked(rows, ext):
        place = lax.broadcasted_iota(jnp.int32, rows.shape, 0)
        first = ext - dp_index * positions
        return jnp.where((place >= first) & (place < first + length), rows, jnp.zeros_like(rows))

    def hop(rows, source, target):
        pairs = [(source * dp + i, target * dp + i) for i in range(dp)]
        pairs += [(target * dp + i, source * dp + i) for i in range(dp)]
        return lax.ppermute(rows, ("section", "dp"), sorted(pairs))

    def after(value, *others):
        return lax.optimization_barrier((value, *others))[0]

    left, right = halo(inputs, ahead[0], dp)
    current = [jnp.concatenate([left[m], inputs[m], right[m]], axis=0) for m in range(micro)]
    kept = [inputs[m] for m in range(micro)]
    grad_halo = None
    for s in range(sections - 1):
        rows = positions + 2 * ahead[s + 1]
        off = ahead[s] - ahead[s + 1]
        d = dil[s]
        for m in range(micro):
            wide_x = current[m].astype(jnp.float32)
            a = act(wide_x, g_conv).astype(jnp.bfloat16)
            conv = matmul(a[off - d : off - d + rows], taps[0])
            conv = conv + matmul(a[off : off + rows], taps[1])
            conv = conv + matmul(a[off + d : off + d + rows], taps[2])
            b = act(conv, g_point).astype(jnp.bfloat16)
            out = wide_x[off : off + rows] + matmul(b, weight_point)
            out = masked(out.astype(jnp.bfloat16), ahead[s + 1])
            if m + 1 < micro:
                current[m + 1] = after(current[m + 1], out)
            elif s == 1:
                grad_halo = halo(after(grad_out, out), wide, dp)
            elif s == 5:
                grad_halo = lax.optimization_barrier((*grad_halo, out))[:2]
            current[m] = hop(out, s, s + 1)
            mine = current[m][ahead[s + 1] : ahead[s + 1] + positions]
            kept[m] = jnp.where(section == s + 1, mine, kept[m])

    left, right = grad_halo
    current = [jnp.concatenate([left[m], grad_out[m], right[m]], axis=0) for m in range(micro)]

    conv_rows = positions + 2 * wide

    def tap_rows(array, start, count, dim):
        return [
            lax.dynamic_slice_in_dim(array, start + (k - 1) * dilation, count, dim)
            for k in range(3)
        ]

    base = back[sections - 1]
    core = slice(outer - base, outer + positions + base)
    x_halos = [halo(kept[m][None], outer, dp) for m in range(micro)]
    a_ext, b_main, x_res, v_res = [], [], [], []

    def residuals(m, *earlier):
        left, right = x_halos[m]
        x_ext = jnp.concatenate([left[0], kept[m], right[0]], axis=0)
        if earlier:
            x_ext = after(x_ext, *earlier)
        x_hat, x_inv = normed(x_ext.astype(jnp.float32))
        a_wide, x_slope = gelu_and_slope(x_hat * g_conv)
        a_ext.append(a_wide.astype(jnp.bfloat16))
        columns = tap_rows(a_ext[m], outer - wide, conv_rows, 0)
        conv = sum(matmul(columns[k], taps[k]) for k in range(3))
        v_hat, v_inv = normed(conv)
        b_wide, v_slope = gelu_and_slope(v_hat * g_point)
        b_main.append(b_wide[wide : wide + positions].astype(jnp.bfloat16))
        x_res.append(lax.optimization_barrier((x_hat[core], x_inv[core], x_slope[core])))
        v_res.append(lax.optimization_barrier((v_hat, v_inv, v_slope)))

    def act_pull(grad, gain, hat, inverse, slope):
        w = grad * slope * gain
        return inverse * (w - hat * jnp.mean(w * hat, axis=-1, keepdims=True))

    y_index = dp_index // nz
    unit = channels // ny

    def to_y(array, k):
        pairs = [(y * nz + z, (y + k) % ny * nz + z) for y in range(ny) for z in range(nz)]
        return lax.ppermute(array, "dp", pairs)

    def y_columns(a_own, b_own, k):
        target = (y_index + k) % ny
        parts = []
        for i in range(3):
            index = 3 * target + i
            start = outer + (index // ny - 1) * dilation
            parts.append(
                lax.dynamic_slice(
                    a_own, (0, start, index % ny * unit), (micro, positions, unit)
                ).reshape(micro * positions, unit)
            )
        return jnp.concatenate(parts + [b_own], axis=1)

    kept_in = [grad_out[m] for m in range(micro)]
    kept_q = [jnp.zeros((positions + 2 * reach, inner), jnp.bfloat16) for m in range(micro)]
    kept_out = [grad_out[m] for m in range(micro)]
    for s in reversed(range(sections)):
        rows = positions + 2 * back[s]
        d = dil[s]
        here = section == s
        ext = back[s + 1]
        outs, qs = [], []
        if s == 2:
            current[0] = lax.optimization_barrier((current[0], *cols))
            cols = current[0][1:]
            current[0] = current[0][0]

        def mix_part(m, e):
            part = slice(wide - ext, wide + positions + ext)
            v_hat, v_inv, v_slope = (r[part] for r in v_res[m])
            grad_b = matmul_t(e, weight_point)
            q = act_pull(grad_b, g_point, v_hat, v_inv, v_slope).astype(jnp.bfloat16)
            mine_q = q[max(ext - reach, 0) : ext + positions + reach]
            if ext < reach:
                mine_q = jnp.pad(mine_q, ((reach - ext, reach - ext), (0, 0)))
            kept_q[m] = jnp.where(here, mine_q, kept_q[m])
            kept_in[m] = jnp.where(here, e[ext : ext + positions], kept_in[m])
            return q

        def conv_part(m, e, q):
            r = matmul_t(q[2 * d : 2 * d + rows], taps[0])
            r = r + matmul_t(q[d : d + rows], taps[1])
            r = r + matmul_t(q[:rows], taps[2])
            part = slice(base - back[s], base + positions + back[s])
            x_hat, x_inv, x_slope = (r_[part] for r_ in x_res[m])
            t = act_pull(r, g_conv, x_hat, x_inv, x_slope)
            out = (e[d : d + rows].astype(jnp.float32) + t).astype(jnp.bfloat16)
            out = masked(out, back[s])
            kept_out[m] = jnp.where(here, out[back[s] : back[s] + positions], kept_out[m])
            return out

        if s > 0:
            for m in range(micro):
                if s == sections - 1:
                    residuals(m, *outs)
                e = current[m]
                if m > 0:
                    e = after(e, outs[m - 1])
                outs.append(conv_part(m, e, mix_part(m, e)))
                current[m] = hop(outs[m], s, s - 1)
        else:
            for m in range(micro):
                qs.append(mix_part(m, after(current[m], *qs)))
            for m in range(micro):
                conv_part(m, current[m], after(qs[m], qs[-1], *outs))
        if s == sections - 2:
            a_own = after(jnp.stack(a_ext), *outs)
            b_own = after(jnp.concatenate(b_main, axis=0), *outs)
            cols = [y_columns(a_own, b_own, 0)]
            cols += [to_y(y_columns(a_own, b_own, k), k) for k in range(1, ny)]

    def contract(left, right):
        return lax.dot_general(
            left, right, (((0,), (0,)), ((), ())), preferred_element_type=jnp.float32
        )

    def swap(array, groups):
        return lax.all_to_all(array, "dp", 0, 0, axis_index_groups=groups)

    e_main = jnp.concatenate(kept_in, axis=0)
    grad_point = 0.0
    for k in range(ny):
        part = lax.dynamic_slice_in_dim(e_main, (y_index + k) % ny * unit, unit, 1)
        part = to_y(part, k) if k else part
        grad_point = grad_point + contract(cols[k][:, 3 * unit :], part)
    point_own = inner // dp
    grad_point = grad_point.reshape(ny, nz, point_own, unit).transpose(1, 0, 2, 3)
    grad_point = grad_point.reshape(nz, inner // nz, unit).astype(jnp.bfloat16)
    point_sum = jnp.sum(swap(grad_point, z_groups).astype(jnp.float32), axis=0)

    q_main = jnp.concatenate([q[reach : reach + positions] for q in kept_q], axis=0)
    grad_conv = contract(cols[0][:, : 3 * unit], q_main)
    for k in range(1, ny):
        grad_conv = grad_conv + contract(cols[k][:, : 3 * unit], to_y(q_main, k))
    grad_conv = grad_conv.astype(jnp.bfloat16)
    own_conv = lax.psum_scatter(
        grad_conv, "dp", scatter_dimension=0, axis_index_groups=z_groups, tiled=True
    )
    own_conv = own_conv.astype(jnp.float32) * norm_scale

    q_late = after(jnp.stack(kept_q), grad_conv)
    e_late = after(e_main, grad_conv)
    flat = micro * positions

    def main_rows(res, start):
        return [jnp.concatenate([r[i][start : start + positions] for r in res]) for i in (0, 2)]

    v_hat, v_slope = main_rows(v_res, wide)
    gain_p = jnp.sum(matmul_t(e_late, weight_point) * v_slope * v_hat, axis=0)
    q_cols = [q.reshape(flat, inner) for q in tap_rows(q_late, reach, positions, 1)]
    r = sum(matmul_t(q_cols[2 - k], taps[k]) for k in range(3))
    x_hat, x_slope = main_rows(x_res, base)
    gain_c = jnp.sum(r * x_slope * x_hat, axis=0)
    gains = jnp.concatenate(
        [gain_c.reshape(dp, channels // dp), gain_p.reshape(dp, inner // dp)], axis=1
    )
    gains = gains.reshape(ny, nz, -1).transpose(1, 0, 2)
    gains = swap(gains, z_groups).sum(0)
    width = gains.shape[1]
    gains = jnp.pad(gains, ((0, 0), (0, unit - width)))[:, None]
    last = jnp.concatenate([point_sum.reshape(ny, point_own, unit), gains], axis=1)
    last = swap(last, y_groups) * norm_scale
    own_point = last[:, :point_own].transpose(1, 0, 2).reshape(point_own, channels)
    gains = last[:, point_own, :width].sum(0)
    return (
        own_conv[None],
        own_point[None],
        gains[: channels // dp][None],
        gains[channels // dp :][None],
        jnp.stack(kept_out)[None],
    )


def solution(mesh):
    return jax.shard_map(
        on_device,
        mesh=mesh,
        in_specs=(
            P(None, "dp", None),
            P(None, "dp", None),
            P("section", None, None),
            P("section", None, None),
            P("section", None),
            P("section", None),
        ),
        out_specs=(
            P("section", "dp", None),
            P("section", "dp", None),
            P("section", "dp"),
            P("section", "dp"),
            P("section", None, "dp", None),
        ),
        check_vma=False,
    )
```

```python
import math

import jax
import jax.numpy as jnp
from jax import lax
from jax.sharding import PartitionSpec as P

EPSILON = 1e-06
Y_CHIPS = 4
GELU_SCALE = math.sqrt(2.0 / math.pi)
GELU_CUBIC = 0.044715


def normed(values):
    inverse = lax.rsqrt(jnp.mean(values * values, axis=-1, keepdims=True) + EPSILON)
    return values * inverse, inverse


def gelu_and_slope(u):
    tanh = jnp.tanh(GELU_SCALE * (u + GELU_CUBIC * u * u * u))
    half = 0.5 * (1.0 + tanh)
    slope = half + 0.5 * u * (1.0 - tanh * tanh) * GELU_SCALE * (1.0 + 3.0 * GELU_CUBIC * u * u)
    return u * half, slope


def act(values, gain):
    hat, unused = normed(values)
    return gelu_and_slope(hat * gain)[0]


def matmul(left, right):
    return lax.dot_general(
        left, right, (((left.ndim - 1,), (0,)), ((), ())), preferred_element_type=jnp.float32
    )


def matmul_t(left, right):
    return lax.dot_general(
        left, right, (((left.ndim - 1,), (1,)), ((), ())), preferred_element_type=jnp.float32
    )


def halo(rows, width, dp):
    left = lax.ppermute(rows[:, -width:], "dp", [(i, i + 1) for i in range(dp - 1)])
    right = lax.ppermute(rows[:, :width], "dp", [(i + 1, i) for i in range(dp - 1)])
    return left, right


def on_device(inputs, grad_out, w_conv, w_point, gain_conv, gain_point):
    micro, positions, channels = inputs.shape
    section = lax.axis_index("section")
    sections = lax.axis_size("section")
    dp_index = lax.axis_index("dp")
    dp = lax.axis_size("dp")
    ny = Y_CHIPS
    nz = dp // ny
    y_groups = [[y * nz + z for y in range(ny)] for z in range(nz)]
    z_groups = [[y * nz + z for z in range(nz)] for y in range(ny)]
    length = positions * dp
    norm_scale = 1.0 / math.sqrt(micro * length)
    dil = [3**s // 2**s for s in range(sections)]
    reach = dil[-1]
    ahead = [sum(dil[s : sections - 1]) for s in range(sections)]
    ahead[0] = -(-ahead[0] // 16) * 16
    back = [sum(dil[:s]) for s in range(sections + 1)]
    wide = back[sections]
    outer = wide + reach
    dilation = sum(jnp.where(section == s, dil[s], 0) for s in range(sections))
    inner = w_conv.shape[2]
    weight_conv = w_conv[0]
    taps = weight_conv.reshape(3, channels, inner)
    weight_point = w_point[0]
    g_conv = gain_conv[0][None]
    g_point = gain_point[0][None]

    def masked(rows, ext):
        place = lax.broadcasted_iota(jnp.int32, rows.shape, 0)
        first = ext - dp_index * positions
        return jnp.where((place >= first) & (place < first + length), rows, jnp.zeros_like(rows))

    def hop(rows, source, target):
        pairs = [(source * dp + i, target * dp + i) for i in range(dp)]
        pairs += [(target * dp + i, source * dp + i) for i in range(dp)]
        return lax.ppermute(rows, ("section", "dp"), sorted(pairs))

    def after(value, *others):
        return lax.optimization_barrier((value, *others))[0]

    left, right = halo(inputs, ahead[0], dp)
    current = [jnp.concatenate([left[m], inputs[m], right[m]], axis=0) for m in range(micro)]
    kept = [inputs[m] for m in range(micro)]
    grad_halo = None
    for s in range(sections - 1):
        rows = positions + 2 * ahead[s + 1]
        off = ahead[s] - ahead[s + 1]
        d = dil[s]
        for m in range(micro):
            wide_x = current[m].astype(jnp.float32)
            a = act(wide_x, g_conv).astype(jnp.bfloat16)
            conv = matmul(a[off - d : off - d + rows], taps[0])
            conv = conv + matmul(a[off : off + rows], taps[1])
            conv = conv + matmul(a[off + d : off + d + rows], taps[2])
            b = act(conv, g_point).astype(jnp.bfloat16)
            out = wide_x[off : off + rows] + matmul(b, weight_point)
            out = masked(out.astype(jnp.bfloat16), ahead[s + 1])
            if m + 1 < micro:
                current[m + 1] = after(current[m + 1], out)
            elif s == 1:
                grad_halo = halo(after(grad_out, out), wide, dp)
            elif s == 5:
                grad_halo = lax.optimization_barrier((*grad_halo, out))[:2]
            current[m] = hop(out, s, s + 1)
            mine = current[m][ahead[s + 1] : ahead[s + 1] + positions]
            kept[m] = jnp.where(section == s + 1, mine, kept[m])

    left, right = grad_halo
    current = [jnp.concatenate([left[m], grad_out[m], right[m]], axis=0) for m in range(micro)]

    conv_rows = positions + 2 * wide

    def tap_rows(array, start, count, dim):
        return [
            lax.dynamic_slice_in_dim(array, start + (k - 1) * dilation, count, dim)
            for k in range(3)
        ]

    x_halos = [halo(kept[m][None], outer, dp) for m in range(micro)]
    a_ext, b_main, x_res, v_res = [], [], [], []

    def residuals(m, *earlier):
        left, right = x_halos[m]
        x_ext = jnp.concatenate([left[0], kept[m], right[0]], axis=0)
        if earlier:
            x_ext = after(x_ext, *earlier)
        x_hat, x_inv = normed(x_ext.astype(jnp.float32))
        a_wide, x_slope = gelu_and_slope(x_hat * g_conv)
        a_ext.append(a_wide.astype(jnp.bfloat16))
        columns = tap_rows(a_ext[m], outer - wide, conv_rows, 0)
        conv = sum(matmul(columns[k], taps[k]) for k in range(3))
        v_hat, v_inv = normed(conv)
        b_wide, v_slope = gelu_and_slope(v_hat * g_point)
        b_main.append(b_wide[wide : wide + positions].astype(jnp.bfloat16))
        x_res.append(lax.optimization_barrier((x_hat, x_inv, x_slope)))
        v_res.append(lax.optimization_barrier((v_hat, v_inv, v_slope)))

    def act_pull(grad, gain, hat, inverse, slope):
        w = grad * slope * gain
        return inverse * (w - hat * jnp.mean(w * hat, axis=-1, keepdims=True))

    y_index = dp_index // nz
    unit = channels // ny

    def to_y(array, k):
        pairs = [(y * nz + z, (y + k) % ny * nz + z) for y in range(ny) for z in range(nz)]
        return lax.ppermute(array, "dp", pairs)

    def y_columns(a_own, b_own, k):
        target = (y_index + k) % ny
        parts = []
        for i in range(3):
            index = 3 * target + i
            start = outer + (index // ny - 1) * dilation
            parts.append(
                lax.dynamic_slice(
                    a_own, (0, start, index % ny * unit), (micro, positions, unit)
                ).reshape(micro * positions, unit)
            )
        return jnp.concatenate(parts + [b_own], axis=1)

    kept_in = [grad_out[m] for m in range(micro)]
    kept_q = [jnp.zeros((positions + 2 * reach, inner), jnp.bfloat16) for m in range(micro)]
    kept_out = [grad_out[m] for m in range(micro)]
    for s in reversed(range(sections)):
        rows = positions + 2 * back[s]
        d = dil[s]
        here = section == s
        ext = back[s + 1]
        outs, qs = [], []
        if s == 2:
            current[0] = lax.optimization_barrier((current[0], *cols))
            cols = current[0][1:]
            current[0] = current[0][0]

        def mix_part(m, e):
            part = slice(wide - ext, wide + positions + ext)
            v_hat, v_inv, v_slope = (r[part] for r in v_res[m])
            grad_b = matmul_t(e, weight_point)
            q = act_pull(grad_b, g_point, v_hat, v_inv, v_slope).astype(jnp.bfloat16)
            mine_q = q[max(ext - reach, 0) : ext + positions + reach]
            if ext < reach:
                mine_q = jnp.pad(mine_q, ((reach - ext, reach - ext), (0, 0)))
            kept_q[m] = jnp.where(here, mine_q, kept_q[m])
            kept_in[m] = jnp.where(here, e[ext : ext + positions], kept_in[m])
            return q

        def conv_part(m, e, q):
            r = matmul_t(q[2 * d : 2 * d + rows], taps[0])
            r = r + matmul_t(q[d : d + rows], taps[1])
            r = r + matmul_t(q[:rows], taps[2])
            part = slice(outer - back[s], outer + positions + back[s])
            x_hat, x_inv, x_slope = (r_[part] for r_ in x_res[m])
            t = act_pull(r, g_conv, x_hat, x_inv, x_slope)
            out = (e[d : d + rows].astype(jnp.float32) + t).astype(jnp.bfloat16)
            out = masked(out, back[s])
            kept_out[m] = jnp.where(here, out[back[s] : back[s] + positions], kept_out[m])
            return out

        if s > 0:
            for m in range(micro):
                if s == sections - 1:
                    residuals(m, *outs)
                e = current[m]
                if m > 0:
                    e = after(e, outs[m - 1])
                outs.append(conv_part(m, e, mix_part(m, e)))
                current[m] = hop(outs[m], s, s - 1)
        else:
            for m in range(micro):
                qs.append(mix_part(m, after(current[m], *qs)))
            for m in range(micro):
                conv_part(m, current[m], after(qs[m], qs[-1], *outs))
        if s == sections - 2:
            a_own = after(jnp.stack(a_ext), *outs)
            b_own = after(jnp.concatenate(b_main, axis=0), *outs)
            cols = [y_columns(a_own, b_own, 0)]
            cols += [to_y(y_columns(a_own, b_own, k), k) for k in range(1, ny)]

    def contract(left, right):
        return lax.dot_general(
            left, right, (((0,), (0,)), ((), ())), preferred_element_type=jnp.float32
        )

    def swap(array, groups):
        return lax.all_to_all(array, "dp", 0, 0, axis_index_groups=groups)

    e_main = jnp.concatenate(kept_in, axis=0)
    q_main = jnp.concatenate([q[reach : reach + positions] for q in kept_q], axis=0)
    e_got, q_got = [], []
    for k in range(ny):
        part = lax.dynamic_slice_in_dim(e_main, (y_index + k) % ny * unit, unit, 1)
        if k == 0:
            both = (part, q_main)
        elif k == 2:
            both = to_y(jnp.concatenate([part, q_main], axis=1), k)
            both = (both[:, :unit], both[:, unit:])
        else:
            both = (to_y(part, k), to_y(q_main, k))
        e_got.append(both[0])
        q_got.append(both[1])
    order = (0, 1, 3, 2)
    grad_point = sum(contract(cols[k][:, 3 * unit :], e_got[k]) for k in order)
    point_own = inner // dp
    grad_point = grad_point.reshape(ny, nz, point_own, unit).transpose(1, 0, 2, 3)
    grad_point = grad_point.reshape(nz, inner // nz, unit).astype(jnp.bfloat16)
    point_sum = jnp.sum(swap(grad_point, z_groups).astype(jnp.float32), axis=0)

    grad_conv = sum(contract(cols[k][:, : 3 * unit], q_got[k]) for k in order)
    grad_conv = grad_conv.astype(jnp.bfloat16)
    own_conv = lax.psum_scatter(
        grad_conv, "dp", scatter_dimension=0, axis_index_groups=z_groups, tiled=True
    )
    own_conv = own_conv.astype(jnp.float32) * norm_scale

    q_late = after(jnp.stack(kept_q), grad_conv)
    e_late = after(e_main, grad_conv)
    flat = micro * positions

    def main_rows(res, start):
        return [jnp.concatenate([r[i][start : start + positions] for r in res]) for i in (0, 2)]

    v_hat, v_slope = main_rows(v_res, wide)
    gain_p = jnp.sum(matmul_t(e_late, weight_point) * v_slope * v_hat, axis=0)
    q_cols = [q.reshape(flat, inner) for q in tap_rows(q_late, reach, positions, 1)]
    r = sum(matmul_t(q_cols[2 - k], taps[k]) for k in range(3))
    x_hat, x_slope = main_rows(x_res, outer)
    gain_c = jnp.sum(r * x_slope * x_hat, axis=0)
    gains = jnp.concatenate(
        [gain_c.reshape(dp, channels // dp), gain_p.reshape(dp, inner // dp)], axis=1
    )
    gains = gains.reshape(ny, nz, -1).transpose(1, 0, 2)
    gains = swap(after(gains, point_sum), z_groups).sum(0)
    width = gains.shape[1]
    gains = jnp.pad(gains, ((0, 0), (0, unit - width)))[:, None]
    last = jnp.concatenate([point_sum.reshape(ny, point_own, unit), gains], axis=1)
    last = swap(last, y_groups) * norm_scale
    own_point = last[:, :point_own].transpose(1, 0, 2).reshape(point_own, channels)
    gains = last[:, point_own, :width].sum(0)
    return (
        own_conv[None],
        own_point[None],
        gains[: channels // dp][None],
        gains[channels // dp :][None],
        jnp.stack(kept_out)[None],
    )


def solution(mesh):
    return jax.shard_map(
        on_device,
        mesh=mesh,
        in_specs=(
            P(None, "dp", None),
            P(None, "dp", None),
            P("section", None, None),
            P("section", None, None),
            P("section", None),
            P("section", None),
        ),
        out_specs=(
            P("section", "dp", None),
            P("section", "dp", None),
            P("section", "dp"),
            P("section", "dp"),
            P("section", None, "dp", None),
        ),
        check_vma=False,
    )
```

```python
import math

import jax
import jax.numpy as jnp
from jax import lax
from jax.sharding import PartitionSpec as P

EPSILON = 1e-06
Y_CHIPS = 4
GELU_SCALE = math.sqrt(2.0 / math.pi)
GELU_CUBIC = 0.044715


def normed(values):
    inverse = lax.rsqrt(jnp.mean(values * values, axis=-1, keepdims=True) + EPSILON)
    return values * inverse, inverse


def gelu_and_slope(u):
    tanh = jnp.tanh(GELU_SCALE * (u + GELU_CUBIC * u * u * u))
    half = 0.5 * (1.0 + tanh)
    slope = half + 0.5 * u * (1.0 - tanh * tanh) * GELU_SCALE * (1.0 + 3.0 * GELU_CUBIC * u * u)
    return u * half, slope


def act(values, gain):
    hat, unused = normed(values)
    return gelu_and_slope(hat * gain)[0]


def matmul(left, right):
    return lax.dot_general(
        left, right, (((left.ndim - 1,), (0,)), ((), ())), preferred_element_type=jnp.float32
    )


def matmul_t(left, right):
    return lax.dot_general(
        left, right, (((left.ndim - 1,), (1,)), ((), ())), preferred_element_type=jnp.float32
    )


def halo(rows, width, dp):
    left = lax.ppermute(rows[:, -width:], "dp", [(i, i + 1) for i in range(dp - 1)])
    right = lax.ppermute(rows[:, :width], "dp", [(i + 1, i) for i in range(dp - 1)])
    return left, right


def on_device(inputs, grad_out, w_conv, w_point, gain_conv, gain_point):
    micro, positions, channels = inputs.shape
    section = lax.axis_index("section")
    sections = lax.axis_size("section")
    dp_index = lax.axis_index("dp")
    dp = lax.axis_size("dp")
    ny = Y_CHIPS
    nz = dp // ny
    y_groups = [[y * nz + z for y in range(ny)] for z in range(nz)]
    z_groups = [[y * nz + z for z in range(nz)] for y in range(ny)]
    length = positions * dp
    norm_scale = 1.0 / math.sqrt(micro * length)
    dil = [3**s // 2**s for s in range(sections)]
    reach = dil[-1]
    ahead = [sum(dil[s : sections - 1]) for s in range(sections)]
    ahead[0] = -(-ahead[0] // 16) * 16
    back = [sum(dil[:s]) for s in range(sections + 1)]
    wide = back[sections]
    outer = wide + reach
    dilation = sum(jnp.where(section == s, dil[s], 0) for s in range(sections))
    inner = w_conv.shape[2]
    weight_conv = w_conv[0]
    taps = weight_conv.reshape(3, channels, inner)
    weight_point = w_point[0]
    g_conv = gain_conv[0][None]
    g_point = gain_point[0][None]

    def masked(rows, ext):
        place = lax.broadcasted_iota(jnp.int32, rows.shape, 0)
        first = ext - dp_index * positions
        return jnp.where((place >= first) & (place < first + length), rows, jnp.zeros_like(rows))

    def hop(rows, source, target):
        pairs = [(source * dp + i, target * dp + i) for i in range(dp)]
        pairs += [(target * dp + i, source * dp + i) for i in range(dp)]
        return lax.ppermute(rows, ("section", "dp"), sorted(pairs))

    def after(value, *others):
        return lax.optimization_barrier((value, *others))[0]

    left, right = halo(inputs, ahead[0], dp)
    current = [jnp.concatenate([left[m], inputs[m], right[m]], axis=0) for m in range(micro)]
    kept = [inputs[m] for m in range(micro)]
    grad_halo = None
    for s in range(sections - 1):
        rows = positions + 2 * ahead[s + 1]
        off = ahead[s] - ahead[s + 1]
        d = dil[s]
        for m in range(micro):
            wide_x = current[m].astype(jnp.float32)
            a = act(wide_x, g_conv).astype(jnp.bfloat16)
            conv = matmul(a[off - d : off - d + rows], taps[0])
            conv = conv + matmul(a[off : off + rows], taps[1])
            conv = conv + matmul(a[off + d : off + d + rows], taps[2])
            b = act(conv, g_point).astype(jnp.bfloat16)
            out = wide_x[off : off + rows] + matmul(b, weight_point)
            out = masked(out.astype(jnp.bfloat16), ahead[s + 1])
            if m + 1 < micro:
                current[m + 1] = after(current[m + 1], out)
            elif s == 1:
                grad_halo = halo(after(grad_out, out), wide, dp)
            elif s == 5:
                grad_halo = lax.optimization_barrier((*grad_halo, out))[:2]
            current[m] = hop(out, s, s + 1)
            mine = current[m][ahead[s + 1] : ahead[s + 1] + positions]
            kept[m] = jnp.where(section == s + 1, mine, kept[m])

    left, right = grad_halo
    current = [jnp.concatenate([left[m], grad_out[m], right[m]], axis=0) for m in range(micro)]

    conv_rows = positions + 2 * wide

    def tap_rows(array, start, count, dim):
        return [
            lax.dynamic_slice_in_dim(array, start + (k - 1) * dilation, count, dim)
            for k in range(3)
        ]

    x_halos = [halo(kept[m][None], outer, dp) for m in range(micro)]
    a_ext, b_main, x_res, v_res = [], [], [], []

    def residuals(m, *earlier):
        left, right = x_halos[m]
        x_ext = jnp.concatenate([left[0], kept[m], right[0]], axis=0)
        if earlier:
            x_ext = after(x_ext, *earlier)
        x_hat, x_inv = normed(x_ext.astype(jnp.float32))
        a_wide, x_slope = gelu_and_slope(x_hat * g_conv)
        a_ext.append(a_wide.astype(jnp.bfloat16))
        columns = tap_rows(a_ext[m], outer - wide, conv_rows, 0)
        conv = sum(matmul(columns[k], taps[k]) for k in range(3))
        v_hat, v_inv = normed(conv)
        b_wide, v_slope = gelu_and_slope(v_hat * g_point)
        b_main.append(b_wide[wide : wide + positions].astype(jnp.bfloat16))
        x_res.append(lax.optimization_barrier((x_hat, x_inv, x_slope)))
        v_res.append(lax.optimization_barrier((v_hat, v_inv, v_slope)))

    def act_pull(grad, gain, hat, inverse, slope):
        w = grad * slope * gain
        return inverse * (w - hat * jnp.mean(w * hat, axis=-1, keepdims=True))

    y_index = dp_index // nz
    unit = channels // ny

    def to_y(array, k):
        pairs = [(y * nz + z, (y + k) % ny * nz + z) for y in range(ny) for z in range(nz)]
        return lax.ppermute(array, "dp", pairs)

    def y_columns(a_own, b_own, k):
        target = (y_index + k) % ny
        parts = []
        for i in range(3):
            index = 3 * target + i
            start = outer + (index // ny - 1) * dilation
            parts.append(
                lax.dynamic_slice(
                    a_own, (0, start, index % ny * unit), (micro, positions, unit)
                ).reshape(micro * positions, unit)
            )
        return jnp.concatenate(parts + [b_own], axis=1)

    kept_in = [grad_out[m] for m in range(micro)]
    kept_q = [jnp.zeros((positions + 2 * reach, inner), jnp.bfloat16) for m in range(micro)]
    kept_out = [grad_out[m] for m in range(micro)]
    for s in reversed(range(sections)):
        rows = positions + 2 * back[s]
        d = dil[s]
        here = section == s
        ext = back[s + 1]
        outs, qs = [], []
        if s == 2:
            current[0] = lax.optimization_barrier((current[0], *cols))
            cols = current[0][1:]
            current[0] = current[0][0]

        def mix_part(m, e):
            part = slice(wide - ext, wide + positions + ext)
            v_hat, v_inv, v_slope = (r[part] for r in v_res[m])
            grad_b = matmul_t(e, weight_point)
            q = act_pull(grad_b, g_point, v_hat, v_inv, v_slope).astype(jnp.bfloat16)
            mine_q = q[max(ext - reach, 0) : ext + positions + reach]
            if ext < reach:
                mine_q = jnp.pad(mine_q, ((reach - ext, reach - ext), (0, 0)))
            kept_q[m] = jnp.where(here, mine_q, kept_q[m])
            kept_in[m] = jnp.where(here, e[ext : ext + positions], kept_in[m])
            return q

        def conv_part(m, e, q):
            r = matmul_t(q[2 * d : 2 * d + rows], taps[0])
            r = r + matmul_t(q[d : d + rows], taps[1])
            r = r + matmul_t(q[:rows], taps[2])
            part = slice(outer - back[s], outer + positions + back[s])
            x_hat, x_inv, x_slope = (r_[part] for r_ in x_res[m])
            t = act_pull(r, g_conv, x_hat, x_inv, x_slope)
            out = (e[d : d + rows].astype(jnp.float32) + t).astype(jnp.bfloat16)
            out = masked(out, back[s])
            kept_out[m] = jnp.where(here, out[back[s] : back[s] + positions], kept_out[m])
            return out

        if s > 0:
            for m in range(micro):
                if s == sections - 1:
                    residuals(m, *outs)
                e = current[m]
                if m > 0:
                    e = after(e, outs[m - 1])
                outs.append(conv_part(m, e, mix_part(m, e)))
                current[m] = hop(outs[m], s, s - 1)
        else:
            for m in range(micro):
                qs.append(mix_part(m, after(current[m], *qs)))
            for m in range(micro):
                conv_part(m, current[m], after(qs[m], qs[-1], *outs))
        if s == sections - 2:
            a_own = after(jnp.stack(a_ext), *outs)
            b_own = after(jnp.concatenate(b_main, axis=0), *outs)
            cols = [y_columns(a_own, b_own, 0)]
            cols += [to_y(y_columns(a_own, b_own, k), k) for k in range(1, ny)]

    def contract(left, right):
        return lax.dot_general(
            left, right, (((0,), (0,)), ((), ())), preferred_element_type=jnp.float32
        )

    def swap(array, groups):
        return lax.all_to_all(array, "dp", 0, 0, axis_index_groups=groups)

    e_main = jnp.concatenate(kept_in, axis=0)
    q_main = jnp.concatenate([q[reach : reach + positions] for q in kept_q], axis=0)
    e_got, q_got = [], []
    for k in range(ny):
        part = lax.dynamic_slice_in_dim(e_main, (y_index + k) % ny * unit, unit, 1)
        if k == 0:
            both = (part, q_main)
        elif k == 2:
            both = to_y(jnp.concatenate([part, q_main], axis=1), k)
            both = (both[:, :unit], both[:, unit:])
        else:
            both = (to_y(part, k), to_y(q_main, k))
        e_got.append(both[0])
        q_got.append(both[1])
    order = (0, 1, 3, 2)

    q_late = after(jnp.stack(kept_q), *kept_out)
    flat = micro * positions

    def main_rows(res, start):
        return [jnp.concatenate([r[i][start : start + positions] for r in res]) for i in (0, 2)]

    v_hat, v_slope = main_rows(v_res, wide)
    e_late = after(e_main, *kept_out)
    gain_p = jnp.sum(matmul_t(e_late, weight_point) * v_slope * v_hat, axis=0)
    q_cols = [q.reshape(flat, inner) for q in tap_rows(q_late, reach, positions, 1)]
    r = sum(matmul_t(q_cols[2 - k], taps[k]) for k in range(3))
    x_hat, x_slope = main_rows(x_res, outer)
    gain_c = jnp.sum(r * x_slope * x_hat, axis=0)
    gains = jnp.concatenate(
        [gain_c.reshape(dp, channels // dp), gain_p.reshape(dp, inner // dp)], axis=1
    )
    width = gains.shape[1]
    gains = gains.reshape(ny, nz, width).transpose(1, 0, 2).reshape(nz, ny * width)
    gain_rows = -(-ny * width // (16 * unit)) * 16
    gains = jnp.pad(gains, ((0, 0), (0, gain_rows * unit - ny * width)))
    gains = gains.reshape(nz, gain_rows, unit).astype(jnp.bfloat16)
    q_got[2], gains = lax.optimization_barrier((q_got[2], gains))

    grad_conv = sum(contract(cols[k][:, : 3 * unit], q_got[k]) for k in order)
    grad_conv = grad_conv.astype(jnp.bfloat16)
    own_conv = lax.psum_scatter(
        grad_conv, "dp", scatter_dimension=0, axis_index_groups=z_groups, tiled=True
    )
    own_conv = own_conv.astype(jnp.float32) * norm_scale

    point_own = inner // dp
    grad_point = sum(
        contract(cols[k][:, 3 * unit :], after(e_got[k], grad_conv) if k == 2 else e_got[k])
        for k in order
    )
    grad_point = grad_point.reshape(ny, nz, point_own, unit).transpose(1, 0, 2, 3)
    grad_point = grad_point.reshape(nz, inner // nz, unit).astype(jnp.bfloat16)
    pack = jnp.concatenate([grad_point, gains], axis=1)
    total = jnp.sum(swap(pack, z_groups).astype(jnp.float32), axis=0)
    gains = total[inner // nz :].reshape(-1)[: ny * width].reshape(ny, 1, width)
    gains = jnp.pad(gains, ((0, 0), (0, 0), (0, unit - width)))
    last = jnp.concatenate([total[: inner // nz].reshape(ny, point_own, unit), gains], axis=1)
    last = swap(last, y_groups) * norm_scale
    own_point = last[:, :point_own].transpose(1, 0, 2).reshape(point_own, channels)
    gains = last[:, point_own, :width].sum(0)
    return (
        own_conv[None],
        own_point[None],
        gains[: channels // dp][None],
        gains[channels // dp :][None],
        jnp.stack(kept_out)[None],
    )


def solution(mesh):
    return jax.shard_map(
        on_device,
        mesh=mesh,
        in_specs=(
            P(None, "dp", None),
            P(None, "dp", None),
            P("section", None, None),
            P("section", None, None),
            P("section", None),
            P("section", None),
        ),
        out_specs=(
            P("section", "dp", None),
            P("section", "dp", None),
            P("section", "dp"),
            P("section", "dp"),
            P("section", None, "dp", None),
        ),
        check_vma=False,
    )
```

```python
import math

import jax
import jax.numpy as jnp
from jax import lax
from jax.sharding import PartitionSpec as P

EPSILON = 1e-06
Y_CHIPS = 4
GELU_SCALE = math.sqrt(2.0 / math.pi)
GELU_CUBIC = 0.044715


def normed(values):
    inverse = lax.rsqrt(jnp.mean(values * values, axis=-1, keepdims=True) + EPSILON)
    return values * inverse, inverse


def gelu_and_slope(u):
    tanh = jnp.tanh(GELU_SCALE * (u + GELU_CUBIC * u * u * u))
    half = 0.5 * (1.0 + tanh)
    slope = half + 0.5 * u * (1.0 - tanh * tanh) * GELU_SCALE * (1.0 + 3.0 * GELU_CUBIC * u * u)
    return u * half, slope


def act(values, gain):
    hat, unused = normed(values)
    return gelu_and_slope(hat * gain)[0]


def matmul(left, right):
    return lax.dot_general(
        left, right, (((left.ndim - 1,), (0,)), ((), ())), preferred_element_type=jnp.float32
    )


def matmul_t(left, right):
    return lax.dot_general(
        left, right, (((left.ndim - 1,), (1,)), ((), ())), preferred_element_type=jnp.float32
    )


def halo(rows, width, dp):
    left = lax.ppermute(rows[:, -width:], "dp", [(i, i + 1) for i in range(dp - 1)])
    right = lax.ppermute(rows[:, :width], "dp", [(i + 1, i) for i in range(dp - 1)])
    return left, right


def on_device(inputs, grad_out, w_conv, w_point, gain_conv, gain_point):
    micro, positions, channels = inputs.shape
    section = lax.axis_index("section")
    sections = lax.axis_size("section")
    dp_index = lax.axis_index("dp")
    dp = lax.axis_size("dp")
    ny = Y_CHIPS
    nz = dp // ny
    y_groups = [[y * nz + z for y in range(ny)] for z in range(nz)]
    z_groups = [[y * nz + z for z in range(nz)] for y in range(ny)]
    length = positions * dp
    norm_scale = 1.0 / math.sqrt(micro * length)
    dil = [3**s // 2**s for s in range(sections)]
    reach = dil[-1]
    ahead = [sum(dil[s : sections - 1]) for s in range(sections)]
    ahead[0] = -(-ahead[0] // 16) * 16
    back = [sum(dil[:s]) for s in range(sections + 1)]
    wide = back[sections]
    outer = wide + reach
    dilation = sum(jnp.where(section == s, dil[s], 0) for s in range(sections))
    inner = w_conv.shape[2]
    weight_conv = w_conv[0]
    taps = weight_conv.reshape(3, channels, inner)
    weight_point = w_point[0]
    g_conv = gain_conv[0][None]
    g_point = gain_point[0][None]

    begin = [dp_index * positions]

    def masked(rows, ext):
        place = lax.broadcasted_iota(jnp.int32, rows.shape, 0)
        first = ext - begin[-1]
        return jnp.where((place >= first) & (place < first + length), rows, jnp.zeros_like(rows))

    def hop(rows, source, target):
        pairs = [(source * dp + i, target * dp + i) for i in range(dp)]
        pairs += [(target * dp + i, source * dp + i) for i in range(dp)]
        return lax.ppermute(rows, ("section", "dp"), sorted(pairs))

    def after(value, *others):
        return lax.optimization_barrier((value, *others))[0]

    left, right = halo(inputs, ahead[0], dp)
    current = [jnp.concatenate([left[m], inputs[m], right[m]], axis=0) for m in range(micro)]
    kept = [inputs[m] for m in range(micro)]
    grad_halo = None
    for s in range(sections - 1):
        rows = positions + 2 * ahead[s + 1]
        off = ahead[s] - ahead[s + 1]
        d = dil[s]
        for m in range(micro):
            wide_x = current[m].astype(jnp.float32)
            a = act(wide_x, g_conv).astype(jnp.bfloat16)
            conv = matmul(a[off - d : off - d + rows], taps[0])
            conv = conv + matmul(a[off : off + rows], taps[1])
            conv = conv + matmul(a[off + d : off + d + rows], taps[2])
            b = act(conv, g_point).astype(jnp.bfloat16)
            out = wide_x[off : off + rows] + matmul(b, weight_point)
            out = masked(out.astype(jnp.bfloat16), ahead[s + 1])
            if m + 1 < micro:
                current[m + 1] = after(current[m + 1], out)
            elif s == 0:
                begin.append(after(begin[0], out))
            elif s == 1:
                grad_halo = halo(after(grad_out, out), wide, dp)
            elif s == 5:
                grad_halo = lax.optimization_barrier((*grad_halo, out))[:2]
            current[m] = hop(out, s, s + 1)
            mine = current[m][ahead[s + 1] : ahead[s + 1] + positions]
            kept[m] = jnp.where(section == s + 1, mine, kept[m])

    left, right = grad_halo
    current = [jnp.concatenate([left[m], grad_out[m], right[m]], axis=0) for m in range(micro)]

    conv_rows = positions + 2 * wide

    def tap_rows(array, start, count, dim):
        return [
            lax.dynamic_slice_in_dim(array, start + (k - 1) * dilation, count, dim)
            for k in range(3)
        ]

    x_halos = [halo(kept[m][None], outer, dp) for m in range(micro)]
    a_ext, b_main, x_res, v_res = [], [], [], []

    def residuals(m, *earlier):
        left, right = x_halos[m]
        x_ext = jnp.concatenate([left[0], kept[m], right[0]], axis=0)
        if earlier:
            x_ext = after(x_ext, *earlier)
        x_hat, x_inv = normed(x_ext.astype(jnp.float32))
        a_wide, x_slope = gelu_and_slope(x_hat * g_conv)
        a_ext.append(a_wide.astype(jnp.bfloat16))
        columns = tap_rows(a_ext[m], outer - wide, conv_rows, 0)
        conv = sum(matmul(columns[k], taps[k]) for k in range(3))
        v_hat, v_inv = normed(conv)
        b_wide, v_slope = gelu_and_slope(v_hat * g_point)
        b_main.append(b_wide[wide : wide + positions].astype(jnp.bfloat16))
        x_res.append(lax.optimization_barrier((x_hat, x_inv, x_slope)))
        v_res.append(lax.optimization_barrier((v_hat, v_inv, v_slope)))

    def act_pull(grad, gain, hat, inverse, slope):
        w = grad * slope * gain
        return inverse * (w - hat * jnp.mean(w * hat, axis=-1, keepdims=True))

    y_index = dp_index // nz
    unit = channels // ny

    def to_y(array, k):
        pairs = [(y * nz + z, (y + k) % ny * nz + z) for y in range(ny) for z in range(nz)]
        return lax.ppermute(array, "dp", pairs)

    def y_columns(a_own, b_own, k):
        target = (y_index + k) % ny
        parts = []
        for i in range(3):
            index = 3 * target + i
            start = outer + (index // ny - 1) * dilation
            parts.append(
                lax.dynamic_slice(
                    a_own, (0, start, index % ny * unit), (micro, positions, unit)
                ).reshape(micro * positions, unit)
            )
        return jnp.concatenate(parts + [b_own], axis=1)

    kept_in = [grad_out[m] for m in range(micro)]
    kept_q = [jnp.zeros((positions + 2 * reach, inner), jnp.bfloat16) for m in range(micro)]
    kept_out = [grad_out[m] for m in range(micro)]
    for s in reversed(range(sections)):
        rows = positions + 2 * back[s]
        d = dil[s]
        here = section == s
        ext = back[s + 1]
        outs, qs = [], []
        if s == 2:
            current[0] = lax.optimization_barrier((current[0], *cols))
            cols = current[0][1:]
            current[0] = current[0][0]

        def mix_part(m, e):
            part = slice(wide - ext, wide + positions + ext)
            v_hat, v_inv, v_slope = (r[part] for r in v_res[m])
            grad_b = matmul_t(e, weight_point)
            q = act_pull(grad_b, g_point, v_hat, v_inv, v_slope).astype(jnp.bfloat16)
            mine_q = q[max(ext - reach, 0) : ext + positions + reach]
            if ext < reach:
                mine_q = jnp.pad(mine_q, ((reach - ext, reach - ext), (0, 0)))
            kept_q[m] = jnp.where(here, mine_q, kept_q[m])
            kept_in[m] = jnp.where(here, e[ext : ext + positions], kept_in[m])
            return q

        def conv_part(m, e, q):
            r = matmul_t(q[2 * d : 2 * d + rows], taps[0])
            r = r + matmul_t(q[d : d + rows], taps[1])
            r = r + matmul_t(q[:rows], taps[2])
            part = slice(outer - back[s], outer + positions + back[s])
            x_hat, x_inv, x_slope = (r_[part] for r_ in x_res[m])
            t = act_pull(r, g_conv, x_hat, x_inv, x_slope)
            out = (e[d : d + rows].astype(jnp.float32) + t).astype(jnp.bfloat16)
            out = masked(out, back[s])
            kept_out[m] = jnp.where(here, out[back[s] : back[s] + positions], kept_out[m])
            return out

        if s > 0:
            for m in range(micro):
                if s == sections - 1:
                    residuals(m, *outs)
                e = current[m]
                if m > 0:
                    e = after(e, outs[m - 1])
                outs.append(conv_part(m, e, mix_part(m, e)))
                current[m] = hop(outs[m], s, s - 1)
        else:
            for m in range(micro):
                qs.append(mix_part(m, after(current[m], *qs)))
            for m in range(micro):
                conv_part(m, current[m], after(qs[m], qs[-1], *outs))
        if s == sections - 2:
            a_own = after(jnp.stack(a_ext), *outs)
            b_own = after(jnp.concatenate(b_main, axis=0), *outs)
            cols = [y_columns(a_own, b_own, 0)]
            cols += [to_y(y_columns(a_own, b_own, k), k) for k in range(1, ny)]

    def contract(left, right):
        return lax.dot_general(
            left, right, (((0,), (0,)), ((), ())), preferred_element_type=jnp.float32
        )

    def swap(array, groups):
        return lax.all_to_all(array, "dp", 0, 0, axis_index_groups=groups)

    e_main = jnp.concatenate(kept_in, axis=0)
    q_main = jnp.concatenate([q[reach : reach + positions] for q in kept_q], axis=0)
    e_got, q_got = [], []
    for k in range(ny):
        part = lax.dynamic_slice_in_dim(e_main, (y_index + k) % ny * unit, unit, 1)
        if k == 0:
            both = (part, q_main)
        elif k == 2:
            both = to_y(jnp.concatenate([part, q_main], axis=1), k)
            both = (both[:, :unit], both[:, unit:])
        else:
            both = (to_y(part, k), to_y(q_main, k))
        e_got.append(both[0])
        q_got.append(both[1])
    order = (0, 1, 3, 2)
    grad_point = sum(contract(cols[k][:, 3 * unit :], e_got[k]) for k in order)
    point_own = inner // dp
    grad_point = grad_point.reshape(ny, nz, point_own, unit).transpose(1, 0, 2, 3)
    grad_point = grad_point.reshape(nz, inner // nz, unit).astype(jnp.bfloat16)
    point_sum = jnp.sum(swap(grad_point, z_groups).astype(jnp.float32), axis=0)

    grad_conv = sum(contract(cols[k][:, : 3 * unit], q_got[k]) for k in order)
    grad_conv = grad_conv.astype(jnp.bfloat16)
    own_conv = lax.psum_scatter(
        grad_conv, "dp", scatter_dimension=0, axis_index_groups=z_groups, tiled=True
    )
    own_conv = own_conv.astype(jnp.float32) * norm_scale

    q_late = after(jnp.stack(kept_q), grad_conv)
    e_late = after(e_main, grad_conv)
    flat = micro * positions

    def main_rows(res, start):
        return [jnp.concatenate([r[i][start : start + positions] for r in res]) for i in (0, 2)]

    v_hat, v_slope = main_rows(v_res, wide)
    gain_p = jnp.sum(matmul_t(e_late, weight_point) * v_slope * v_hat, axis=0)
    q_cols = [q.reshape(flat, inner) for q in tap_rows(q_late, reach, positions, 1)]
    r = sum(matmul_t(q_cols[2 - k], taps[k]) for k in range(3))
    x_hat, x_slope = main_rows(x_res, outer)
    gain_c = jnp.sum(r * x_slope * x_hat, axis=0)
    gains = jnp.concatenate(
        [gain_c.reshape(dp, channels // dp), gain_p.reshape(dp, inner // dp)], axis=1
    )
    gains = gains.reshape(ny, nz, -1).transpose(1, 0, 2)
    gains = swap(after(gains, point_sum), z_groups).sum(0)
    width = gains.shape[1]
    gains = jnp.pad(gains, ((0, 0), (0, unit - width)))[:, None]
    last = jnp.concatenate([point_sum.reshape(ny, point_own, unit), gains], axis=1)
    last = swap(last, y_groups) * norm_scale
    own_point = last[:, :point_own].transpose(1, 0, 2).reshape(point_own, channels)
    gains = last[:, point_own, :width].sum(0)
    return (
        own_conv[None],
        own_point[None],
        gains[: channels // dp][None],
        gains[channels // dp :][None],
        jnp.stack(kept_out)[None],
    )


def solution(mesh):
    return jax.shard_map(
        on_device,
        mesh=mesh,
        in_specs=(
            P(None, "dp", None),
            P(None, "dp", None),
            P("section", None, None),
            P("section", None, None),
            P("section", None),
            P("section", None),
        ),
        out_specs=(
            P("section", "dp", None),
            P("section", "dp", None),
            P("section", "dp"),
            P("section", "dp"),
            P("section", None, "dp", None),
        ),
        check_vma=False,
    )
```
